32 devices in a mesh: tm: 2 (over y), aux: 16 (over z, x, core).
Axes of the slice: x: 2, y: 2, z: 4, core: 2. Of those that a mesh axis runs over, the one named last changes fastest.
Arguments:
- green: bfloat16 [4, 1024, 1024], P('tm'), may hold values from -4 to 4
- factors: bfloat16 [4096, 1024], P('aux'), may hold values from -0.1875 to 0.1875
- pattern: int32 [32, 8], P('aux'), may hold values 0 or 1
- coulomb: float32 [4096], P('aux'), may hold values from 0.5 to 2
Outputs:
- sigma: float32 [1024, 4, 1024], P('aux', 'tm')
The draws below stay inside these ranges and needn't reach their ends.
All inputs are finite; a program needn't handle non-finite values. No bound on the sum of `pattern` on one device may be relied on, other than what follows from the above.
Results may differ from the reference program's by a relative error of at most 0.006.
Values may be sent and summed in bfloat16 or wider, within the bound.
A program may use at most 64 MiB of HBM per device.

```python
import math
import jax
import jax.numpy as jnp
from jax import lax

ORB = 1024
AUX = 4096
BLOCK = 128
TIMES = 4


def plant(result, own_key, smallest, top_value):
    dims = result.shape
    index_at = [jax.random.randint(jax.random.fold_in(own_key, axis), (), 0, dims[axis]) for axis in range(len(dims))]
    result = result.at[tuple(index_at)].set(smallest)
    longest = dims.index(max(dims))
    index_at[longest] = (index_at[longest] + 1) % dims[longest]
    return result.at[tuple(index_at)].set(top_value)


def block_levels(key, shape, shards, smallest, top_value):
    loudness, own = 1.0, jax.random.fold_in(key, 6)
    for axis_at, blocks in shards:
        heights = jnp.exp(jax.random.uniform(jax.random.fold_in(own, axis_at), (blocks,), jnp.float32, smallest / len(shards), top_value / len(shards)))
        loudness = loudness * jnp.repeat(heights, shape[axis_at] // blocks).reshape([-1 if axis == axis_at else 1 for axis in range(len(shape))])
    return loudness


def normal_values(rng, dims, spread, reach, pieces=(), kind=jnp.bfloat16):
    entries = jax.random.normal(rng, dims, jnp.float32) * spread
    if len(pieces) > 0:
        entries = block_levels(rng, dims, pieces, -0.22, 0.18) * entries
    return jnp.clip(entries, min=-reach, max=reach).astype(kind)


def setup_inputs(seed: int = 0) -> dict:
    splits = jax.random.split(jax.random.key(seed), 5)
    return {
        "green": normal_values(splits[0], (TIMES, ORB, ORB), 0.45, 4.0, ((0, 2),)),
        "factors": normal_values(splits[1], (AUX, ORB), ORB ** -0.5, 0.1875, ((0, 16),)),
        "pattern": plant((jax.random.randint(splits[2], (AUX // BLOCK, ORB // BLOCK), 0, 4) < 3).astype(jnp.int32), jax.random.fold_in(splits[2], 1), 0, 1),
        "coulomb": jnp.clip(jnp.exp(math.log(2.0) - 1.3862944 * jax.random.uniform(splits[3], (AUX,), jnp.float32) ** block_levels(splits[3], (AUX,), ((0, 16),), -0.2, 0.2)), 0.5, 2.0),
    }


def reference(green, factors, pattern, coulomb):
    mask = jnp.repeat(jnp.repeat(pattern, BLOCK, axis=0), BLOCK, axis=1)
    masked = factors * mask.astype(factors.dtype)

    def project(gmat):
        left = jnp.dot(masked, gmat, preferred_element_type=jnp.float32).astype(jnp.bfloat16)
        right = jnp.dot(masked, gmat.T, preferred_element_type=jnp.float32).astype(jnp.bfloat16)
        return left, right

    lefts, rights = lax.map(project, green)
    mirrored = jnp.roll(rights, TIMES // 2, axis=0)

    def self_energy(pair):
        left, right = pair
        aux_green = jnp.dot(left, masked.T, preferred_element_type=jnp.float32)
        mirror = jnp.dot(right, masked.T, preferred_element_type=jnp.float32)
        chi = -aux_green * mirror
        kernel = (aux_green * coulomb[:, None] * chi * coulomb[None, :]).astype(jnp.bfloat16)
        carried = jnp.dot(kernel, masked, preferred_element_type=jnp.float32).astype(jnp.bfloat16)
        return -jnp.dot(masked.T, carried, preferred_element_type=jnp.float32)

    sigma = lax.map(self_energy, (lefts, mirrored))
    return jnp.transpose(sigma, (1, 0, 2))
```

```python
import functools

import jax
import jax.numpy as jnp
from jax import lax
from jax.experimental import pallas as pl
from jax.experimental.pallas import tpu as pltpu
from jax.sharding import PartitionSpec as P

MESH = pl.DeviceIdType.MESH
F32, BF16 = jnp.float32, jnp.bfloat16


def turned(p):
    return p + lax.div(p, 2) * (1 - 2 * lax.rem(p, 2))


def dot(a, b, da, db):
    return lax.dot_general(a, b, (((da,), (db,)), ((), ())), preferred_element_type=F32)


def kernel(cfg, pattern, factors, coul, green_hbm, out, own, rows, weights, green, left_right,
           own_right, cp, kern, sig, csend, crecv, xsend, xrecv, zsend, zrecv, fin,
           gsem, ring_s, ring_r, x_s, x_r, cc_s, cc_r, cx_s, cx_r, tm_s, tm_r,
           rc_s, rc_r, rx_s, rx_r, rz_s, rz_r):
    Z, X, JH = cfg
    T, O = green.shape[0], green.shape[1]
    R = own.shape[0]
    JW = O // JH
    OUT = out.shape[1]
    tms = lax.axis_size("tm")
    a, tmi = lax.axis_index("aux"), lax.axis_index("tm")
    c = lax.rem(a, 2)
    x = lax.rem(lax.div(a, 2), X)
    z = lax.div(a, 2 * X)
    pos = turned(z)

    def dev(z_, x_, c_):
        return (z_ * X + x_) * 2 + c_

    def xo(e):
        return lax.rem(x + e, X)

    def zo(f):
        return lax.rem(z + f, Z)

    partner = lax.rem(tmi + tms // 2, tms)
    sibling = dev(z, x, 1 - c)
    sent = []

    def send(src, dst, s, r, **where):
        copy = pltpu.make_async_remote_copy(
            src_ref=src, dst_ref=dst, send_sem=s, recv_sem=r,
            device_id=where, device_id_type=MESH)
        copy.start()
        sent.append(copy)
        return copy

    loads = [pltpu.make_async_copy(green_hbm.at[t], green.at[t], gsem.at[t]) for t in range(T)]
    for copy in loads:
        copy.start()

    here = pl.multiple_of(a * R, R)
    brows = R // pattern.shape[0]
    bcols = O // pattern.shape[1]
    for i in range(pattern.shape[0]):
        for j in range(pattern.shape[1]):
            rs, cs = pl.ds(i * brows, brows), pl.ds(j * bcols, bcols)
            own[rs, cs] = (factors[rs, cs].astype(F32) * pattern[i, j].astype(F32)).astype(BF16)
    rows[pl.ds(here, R), :] = own[...]
    weights[a] = coul[...]
    cp[...] = jnp.transpose(jnp.broadcast_to(coul[...], (R, R)))

    barrier = pltpu.get_barrier_semaphore()
    friends = [{"aux": dev(zo(f), x, c)} for f in range(1, Z)]
    friends += [{"aux": dev(z, xo(e), c)} for e in range(1, X)]
    friends += [{"aux": sibling}, {"tm": partner}]
    for where in friends:
        pl.semaphore_signal(barrier, inc=1, device_id=where, device_id_type=MESH)
    pl.semaphore_wait(barrier, len(friends))

    nextd = dev(turned(lax.rem(pos + 1, Z)), x, c)

    def col_owner(k):
        return dev(turned(lax.rem(pos + Z - k, Z)), x, c)

    def xin_owner(k, e):
        return dev(turned(lax.rem(pos + Z - k, Z)), lax.rem(x + X - e, X), c)

    def pass_on(owner, s, r, to, first=False):
        at = pl.ds(pl.multiple_of(owner * R, R), R)
        src_rows = own if first else rows.at[at]
        src_w = coul if first else weights.at[owner]
        return [send(src_rows, rows.at[at], s.at[0], r.at[0], aux=to),
                send(src_w, weights.at[owner], s.at[1], r.at[1], aux=to)]

    ring, xs, ccs, cxs = {}, {}, {}, {}

    def wait_all(copies):
        for copy in copies:
            copy.wait_recv()

    def col_ready(k):
        if k > 0:
            wait_all(ring[k])
        owner = col_owner(k)
        if k < Z - 1:
            ring[k + 1] = pass_on(owner, ring_s.at[k], ring_r.at[k], nextd, k == 0)
        for e in range(1, X):
            xs[k, e] = pass_on(owner, x_s.at[k, e - 1], x_r.at[k, e - 1], dev(z, xo(e), c), k == 0)
        ccs[k] = pass_on(owner, cc_s.at[k], cc_r.at[k], sibling, k == 0)

    def xin_ready(k):
        for e in range(1, X):
            wait_all(xs[k, e])
            cxs[k, e] = pass_on(xin_owner(k, e), cx_s.at[k, e - 1], cx_r.at[k, e - 1], sibling)

    waited = set()

    def once(key, copies):
        if key not in waited:
            waited.add(key)
            wait_all(copies)

    def blocks(owner, ts):
        def one(i, carry):
            who = owner - c + lax.rem(c + lax.div(i, len(ts)), 2)
            t = ts[0] + lax.rem(i, len(ts))
            at = pl.ds(pl.multiple_of(who * R, R), R)
            both = dot(left_right[t], rows[at, :], 1, 1)
            ag, mirror = both[:R], both[R:]
            kern[t, :, at] = (ag * ag * mirror * (cp[...] * weights[who])).astype(BF16)
            return carry
        lax.fori_loop(0, 2 * len(ts), one, 0)

    def do_col(k, ts):
        once(("c", k), ccs[k])
        blocks(col_owner(k), ts)

    def do_xin(k, ts):
        for e in range(1, X):
            once(("x", k, e), cxs[k, e])
            blocks(xin_owner(k, e), ts)

    rights = {}

    def project_right(t):
        loads[t].wait()

        def one(j, carry):
            at = pl.ds(pl.multiple_of(j * 256, 256), 256)
            own_right[t, :, at] = dot(own[...], green[t, at, :], 1, 1).astype(BF16)
            return carry
        lax.fori_loop(0, O // 256, one, 0)
        rights[t] = send(own_right.at[t], left_right.at[t, pl.ds(R, R)], tm_s.at[t], tm_r.at[t],
                         tm=partner)

    def project_left(t):
        def one(j, carry):
            at = pl.ds(pl.multiple_of(j * 256, 256), 256)
            left_right[t, pl.ds(0, R), at] = dot(own[...], green[t, :, at], 1, 0).astype(BF16)
            return carry
        lax.fori_loop(0, O // 256, one, 0)

    col_ready(0)
    for t in range(T):
        project_right(t)
    for t in range(T):
        project_left(t)
    col_ready(1)
    xin_ready(0)
    rights[0].wait_recv()
    do_col(0, (0,))
    do_col(1, (0,))
    do_xin(0, (0,))
    col_ready(2)
    xin_ready(1)
    rest = tuple(range(1, T))
    for t in rest:
        rights[t].wait_recv()
    do_col(0, rest)
    do_col(1, rest)
    do_xin(0, rest)
    every = tuple(range(T))
    do_col(2, every)
    for k in range(3, Z):
        col_ready(k)
        xin_ready(k - 1)
        do_xin(k - 2, every)
        do_col(k, every)
    do_xin(Z - 2, every)
    xin_ready(Z - 1)
    do_xin(Z - 1, every)

    pairs = Z * X
    cross, xc, zc = {}, {}, {}

    def stage_a(q):
        t, j0 = q // JH, (q % JH) * JW

        def one(j, carry):
            at = pl.ds(pl.multiple_of(j0 + j * 256, 256), 256)
            carried = dot(kern[t], rows[:, at], 1, 0).astype(BF16)
            to = pl.ds(pl.multiple_of(j * 256, 256), 256)
            sig[q, :, to] = dot(own[...], carried, 0, 0)
            return carry
        lax.fori_loop(0, JW // 256, one, 0)
        for g in range(pairs):
            at = pl.ds(pl.multiple_of((g * 2 + 1 - c) * OUT, OUT), OUT)
            csend[q, g] = sig[q, at, :].astype(BF16)
        cross[q] = send(csend.at[q], crecv.at[q], rc_s.at[q], rc_r.at[q], aux=sibling)

    def summed(q, g):
        at = pl.ds(pl.multiple_of((g * 2 + c) * OUT, OUT), OUT)
        return sig[q, at, :] + crecv[q, g].astype(F32)

    def stage_b(q):
        cross[q].wait_recv()
        for e in range(1, X):
            for zz in range(Z):
                xsend[q, e - 1, zz] = summed(q, zz * X + xo(e)).astype(BF16)
            xc[q, e] = send(xsend.at[q, e - 1], xrecv.at[q, e - 1], rx_s.at[q, e - 1],
                            rx_r.at[q, e - 1], aux=dev(z, xo(e), c))

    def stage_c(q):
        for e in range(1, X):
            xc[q, e].wait_recv()
        for f in list(range(1, Z)) + [0]:
            value = summed(q, zo(f) * X + x)
            for e in range(1, X):
                value = value + xrecv[q, e - 1, zo(f)].astype(F32)
            if f == 0:
                fin[q] = value
            else:
                zsend[q, f - 1] = value.astype(BF16)
                zc[q, f] = send(zsend.at[q, f - 1], zrecv.at[q, f - 1], rz_s.at[q, f - 1],
                                rz_r.at[q, f - 1], aux=dev(zo(f), x, c))

    def stage_d(q):
        value = fin[q]
        for f in range(1, Z):
            zc[q, f].wait_recv()
            value = value + zrecv[q, f - 1].astype(F32)
        out[q // JH, :, pl.ds((q % JH) * JW, JW)] = value

    Q = T * JH
    stage_a(0)
    for q in range(1, Q):
        stage_a(q)
        stage_b(q - 1)
    stage_b(Q - 1)
    stage_c(0)
    for q in range(1, Q):
        stage_c(q)
        stage_d(q - 1)
    stage_d(Q - 1)
    for copy in sent:
        copy.wait_send()


def local(green, factors, pattern, coulomb):
    n = lax.axis_size("aux")
    T, O, _ = green.shape
    R = factors.shape[0]
    A = n * R
    chips = n // 2
    Z = 4
    X = chips // Z
    JH = 2
    JW = O // JH
    Q = T * JH
    OUT = O // n
    dma = pltpu.SemaphoreType.DMA
    vm = pltpu.VMEM
    scratch = [
        vm((R, O), BF16), vm((A, O), BF16), vm((n, 1, R), F32), vm((T, O, O), BF16),
        vm((T, 2 * R, O), BF16), vm((T, R, O), BF16), vm((R, R), F32), vm((T, R, A), BF16),
        vm((Q, O, JW), F32), vm((Q, chips, OUT, JW), BF16), vm((Q, chips, OUT, JW), BF16),
        vm((Q, X - 1, Z, OUT, JW), BF16), vm((Q, X - 1, Z, OUT, JW), BF16),
        vm((Q, Z - 1, OUT, JW), BF16), vm((Q, Z - 1, OUT, JW), BF16), vm((Q, OUT, JW), F32),
        dma((T,)),
        dma((Z - 1, 2)), dma((Z - 1, 2)),
        dma((Z, X - 1, 2)), dma((Z, X - 1, 2)),
        dma((Z, 2)), dma((Z, 2)),
        dma((Z, X - 1, 2)), dma((Z, X - 1, 2)),
        dma((T,)), dma((T,)),
        dma((Q,)), dma((Q,)),
        dma((Q, X - 1)), dma((Q, X - 1)),
        dma((Q, Z - 1)), dma((Q, Z - 1)),
    ]
    vmem = pl.BlockSpec(memory_space=pltpu.VMEM)
    result = pl.pallas_call(
        functools.partial(kernel, (Z, X, JH)),
        out_shape=jax.ShapeDtypeStruct((T, OUT, O), F32),
        in_specs=[pl.BlockSpec(memory_space=pltpu.SMEM), vmem, vmem,
                  pl.BlockSpec(memory_space=pl.ANY)],
        out_specs=vmem,
        scratch_shapes=scratch,
        compiler_params=pltpu.CompilerParams(
            collective_id=0, has_side_effects=True, vmem_limit_bytes=60 * 2**20),
    )(pattern, factors, coulomb.reshape(1, R), green)
    return jnp.transpose(result, (1, 0, 2))


def solution(mesh):
    in_specs = (P("tm", None, None), P("aux", None), P("aux", None), P("aux"))
    out_specs = P("aux", "tm", None)
    return jax.shard_map(local, mesh=mesh, in_specs=in_specs, out_specs=out_specs, check_vma=False)
```

```python
import functools

import jax
import jax.numpy as jnp
from jax import lax
from jax.experimental import pallas as pl
from jax.experimental.pallas import tpu as pltpu
from jax.sharding import PartitionSpec as P

MESH = pl.DeviceIdType.MESH
F32, BF16 = jnp.float32, jnp.bfloat16


def turned(p):
    return p + lax.div(p, 2) * (1 - 2 * lax.rem(p, 2))


def dot(a, b, da, db):
    return lax.dot_general(a, b, (((da,), (db,)), ((), ())), preferred_element_type=F32)


def kernel(cfg, pattern, factors, coul, green_hbm, out, own, rows, weights, green, left_right,
           own_right, cp, kern, sig, csend, crecv, xsend, xrecv, zsend, zrecv, fin,
           gsem, ring_s, ring_r, x_s, x_r, y_s, y_r, cc_s, cc_r, cx_s, cx_r,
           wring_s, wring_r, wx_s, wx_r, wcc_s, wcc_r, wcx_s, wcx_r, tm_s, tm_r,
           rc_s, rc_r, rx_s, rx_r, rz_s, rz_r):
    Z, X, JH, H = cfg
    T, O = green.shape[0], green.shape[1]
    R = own.shape[0]
    JW = O // JH
    OUT = out.shape[1]
    tms = lax.axis_size("tm")
    a, tmi = lax.axis_index("aux"), lax.axis_index("tm")
    c = lax.rem(a, 2)
    x = lax.rem(lax.div(a, 2), X)
    z = lax.div(a, 2 * X)
    pos = turned(z)

    def dev(z_, x_, c_):
        return (z_ * X + x_) * 2 + c_

    def xo(e):
        return lax.rem(x + e, X)

    def zo(f):
        return lax.rem(z + f, Z)

    partner = lax.rem(tmi + tms // 2, tms)
    plane = lax.rem(tmi, 2)
    mate = tmi + 1 - 2 * plane
    sibling = dev(z, x, 1 - c)
    sent = []

    def send(src, dst, s, r, **where):
        copy = pltpu.make_async_remote_copy(
            src_ref=src, dst_ref=dst, send_sem=s, recv_sem=r,
            device_id=where, device_id_type=MESH)
        copy.start()
        sent.append(copy)
        return copy

    loads = [pltpu.make_async_copy(green_hbm.at[t], green.at[t], gsem.at[t]) for t in range(T)]
    for copy in loads:
        copy.start()

    here = pl.multiple_of(a * R, R)
    brows = R // pattern.shape[0]
    bcols = O // pattern.shape[1]
    for i in range(pattern.shape[0]):
        for j in range(pattern.shape[1]):
            rs, cs = pl.ds(i * brows, brows), pl.ds(j * bcols, bcols)
            own[rs, cs] = (factors[rs, cs].astype(F32) * pattern[i, j].astype(F32)).astype(BF16)
    rows[pl.ds(here, R), :] = own[...]
    weights[a] = coul[...]
    cp[...] = jnp.transpose(jnp.broadcast_to(coul[...], (R, R)))

    barrier = pltpu.get_barrier_semaphore()
    friends = [{"aux": dev(zo(f), x, c)} for f in range(1, Z)]
    friends += [{"aux": dev(z, xo(e), c)} for e in range(1, X)]
    friends += [{"aux": sibling}, {"tm": partner}]
    if tms > 2 and tms % 2 == 0:
        friends += [{"tm": mate}]
    for where in friends:
        pl.semaphore_signal(barrier, inc=1, device_id=where, device_id_type=MESH)
    pl.semaphore_wait(barrier, len(friends))

    nextd = dev(turned(lax.rem(pos + 1, Z)), x, c)
    PR = R // H
    shared = ()

    def col_owner(k):
        return dev(turned(lax.rem(pos + Z - k, Z)), x, c)

    def xin_owner(k, e):
        return dev(turned(lax.rem(pos + Z - k, Z)), lax.rem(x + X - e, X), c)

    def pass_piece(owner, h, s, r, first=False, **where):
        at = pl.ds(pl.multiple_of(owner * R + h * PR, PR), PR)
        src = own.at[pl.ds(pl.multiple_of(h * PR, PR), PR)] if first else rows.at[at]
        return send(src, rows.at[at], s, r, **where)

    def pass_weight(owner, s, r, first=False, **where):
        return send(coul if first else weights.at[owner], weights.at[owner], s, r, **where)

    ring, xs, ys, ccs, cxs = {}, {}, {}, {}, {}
    wring, wxs, wccs, wcxs = {}, {}, {}, {}

    def wait_all(copies):
        for copy in copies:
            copy.wait_recv()

    def col(k, h):
        if k > 0:
            ring[k, h].wait_recv()
            if h == 0:
                wring[k].wait_recv()
        owner, first = col_owner(k), k == 0
        if k < Z - 1:
            ring[k + 1, h] = pass_piece(owner, h, ring_s.at[k, h], ring_r.at[k, h], first, aux=nextd)
        for e in range(1, X):
            to = dev(z, xo(e), c)
            if k not in shared:
                xs[k, e, h] = pass_piece(owner, h, x_s.at[k, e - 1, h], x_r.at[k, e - 1, h], first,
                                         aux=to)
            elif h % 2:
                i = h // 2
                xs[k, e, i] = pass_piece(owner, 2 * i + plane, x_s.at[k, e - 1, i],
                                         x_r.at[k, e - 1, i], first, aux=to)
        ccs.setdefault(k, []).append(
            pass_piece(owner, h, cc_s.at[k, h], cc_r.at[k, h], first, aux=sibling))
        if h == 0:
            if k < Z - 1:
                wring[k + 1] = pass_weight(owner, wring_s.at[k], wring_r.at[k], first, aux=nextd)
            for e in range(1, X):
                wxs[k, e] = pass_weight(owner, wx_s.at[k, e - 1], wx_r.at[k, e - 1], first,
                                        aux=dev(z, xo(e), c))
            ccs[k].append(pass_weight(owner, wcc_s.at[k], wcc_r.at[k], first, aux=sibling))

    def xin(k, i):
        for e in range(1, X):
            owner = xin_owner(k, e)
            xs[k, e, i].wait_recv()
            h, n = i, i
            if k in shared:
                h, n = 2 * i + plane, 2 * i
                ys[k, e, i] = pass_piece(owner, h, y_s.at[k, e - 1, i], y_r.at[k, e - 1, i], tm=mate)
            mine = cxs.setdefault((k, e), [])
            mine.append(pass_piece(owner, h, cx_s.at[k, e - 1, n], cx_r.at[k, e - 1, n], aux=sibling))
            if i == 0:
                wxs[k, e].wait_recv()
                mine.append(pass_weight(owner, wcx_s.at[k, e - 1], wcx_r.at[k, e - 1], aux=sibling))

    def yin(k, i):
        for e in range(1, X):
            ys[k, e, i].wait_recv()
            cxs[k, e].append(
                pass_piece(xin_owner(k, e), 2 * i + 1 - plane, cx_s.at[k, e - 1, 2 * i + 1],
                           cx_r.at[k, e - 1, 2 * i + 1], aux=sibling))

    waited = set()

    def once(key, copies):
        if key not in waited:
            waited.add(key)
            wait_all(copies)

    def blocks(owner, ts):
        def one(i, carry):
            who = owner - c + lax.rem(c + lax.div(i, len(ts)), 2)
            t = ts[0] + lax.rem(i, len(ts))
            at = pl.ds(pl.multiple_of(who * R, R), R)
            both = dot(left_right[t], rows[at, :], 1, 1)
            ag, mirror = both[:R], both[R:]
            kern[t, :, at] = (ag * ag * mirror * (cp[...] * weights[who])).astype(BF16)
            return carry
        lax.fori_loop(0, 2 * len(ts), one, 0)

    def do_col(k, ts):
        once(("c", k), ccs[k])
        blocks(col_owner(k), ts)

    def do_xin(k, ts):
        for e in range(1, X):
            once(("x", k, e), cxs[k, e])
            blocks(xin_owner(k, e), ts)

    rights = {}

    def project_right(t):
        loads[t].wait()

        def one(j, carry):
            at = pl.ds(pl.multiple_of(j * 256, 256), 256)
            own_right[t, :, at] = dot(own[...], green[t, at, :], 1, 1).astype(BF16)
            return carry
        lax.fori_loop(0, O // 256, one, 0)
        rights[t] = send(own_right.at[t], left_right.at[t, pl.ds(R, R)], tm_s.at[t], tm_r.at[t],
                         tm=partner)

    def project_left(t):
        def one(j, carry):
            at = pl.ds(pl.multiple_of(j * 256, 256), 256)
            left_right[t, pl.ds(0, R), at] = dot(own[...], green[t, :, at], 1, 0).astype(BF16)
            return carry
        lax.fori_loop(0, O // 256, one, 0)

    for h in range(H):
        col(0, h)
    for t in range(T):
        project_right(t)
    for t in range(T):
        project_left(t)

    rest, every = tuple(range(1, T)), tuple(range(T))
    todo = []

    def plan(when, what, *args):
        todo.append((when, len(todo), what, args))

    lag = 0.7
    for k in range(1, Z):
        for h in range(H):
            plan((k - 1) * H + h + 1 + lag * k, col, k, h)
    last = 0.0
    for k in range(Z):
        if k in shared:
            for i in range(H // 2):
                ready = (k - 1) * H + 2 * i + 2 + lag * k
                last = max(last + 1, ready + 1 + lag)
                plan(last, xin, k, i)
                plan(max(last + 1 + lag, 11.7 + i), yin, k, i)
        else:
            for i in range(H):
                last = k * H + i + 1 + lag
                plan(last, xin, k, i)
    plan(6.5, lambda: rights[0].wait_recv())
    plan(6.6, do_col, 0, (0,))
    plan(6.7, do_col, 1, (0,))
    plan(6.8, do_xin, 0, (0,))
    plan(9.3, do_xin, 1, (0,))
    plan(9.6, do_col, 2, (0,))
    plan(10.6, lambda: [rights[t].wait_recv() for t in rest])
    plan(10.61, do_col, 0, rest)
    plan(10.8, do_col, 1, rest)
    plan(11.2, do_xin, 0, rest)
    plan(11.9, do_xin, 1, rest)
    plan(12.3, do_col, 2, rest)
    tail = 13.3
    for k in range(2, Z):
        if k > 2:
            plan(max(tail, (k - 1) * H + H + lag * k + 0.5), do_col, k, every)
        full = max([w for w, _, f, g in todo if f in (xin, yin) and g[0] == k])
        plan(full + 0.4, do_xin, k, every)
    for _, _, what, args in sorted(todo, key=lambda item: item[:2]):
        what(*args)

    pairs = Z * X
    cross, xc, zc = {}, {}, {}

    def stage_a(q):
        t, j0 = q // JH, (q % JH) * JW

        def one(j, carry):
            at = pl.ds(pl.multiple_of(j0 + j * 256, 256), 256)
            carried = dot(kern[t], rows[:, at], 1, 0).astype(BF16)
            to = pl.ds(pl.multiple_of(j * 256, 256), 256)
            sig[q, :, to] = dot(own[...], carried, 0, 0)
            return carry
        lax.fori_loop(0, JW // 256, one, 0)
        for g in range(pairs):
            at = pl.ds(pl.multiple_of((g * 2 + 1 - c) * OUT, OUT), OUT)
            csend[q, g] = sig[q, at, :].astype(BF16)
        cross[q] = send(csend.at[q], crecv.at[q], rc_s.at[q], rc_r.at[q], aux=sibling)

    def summed(q, g):
        at = pl.ds(pl.multiple_of((g * 2 + c) * OUT, OUT), OUT)
        return sig[q, at, :] + crecv[q, g].astype(F32)

    def stage_b(q):
        cross[q].wait_recv()
        for e in range(1, X):
            for zz in range(Z):
                xsend[q, e - 1, zz] = summed(q, zz * X + xo(e)).astype(BF16)
            xc[q, e] = send(xsend.at[q, e - 1], xrecv.at[q, e - 1], rx_s.at[q, e - 1],
                            rx_r.at[q, e - 1], aux=dev(z, xo(e), c))

    def stage_c(q):
        for e in range(1, X):
            xc[q, e].wait_recv()
        for f in list(range(1, Z)) + [0]:
            value = summed(q, zo(f) * X + x)
            for e in range(1, X):
                value = value + xrecv[q, e - 1, zo(f)].astype(F32)
            if f == 0:
                fin[q] = value
            else:
                zsend[q, f - 1] = value.astype(BF16)
                zc[q, f] = send(zsend.at[q, f - 1], zrecv.at[q, f - 1], rz_s.at[q, f - 1],
                                rz_r.at[q, f - 1], aux=dev(zo(f), x, c))

    def stage_d(q):
        value = fin[q]
        for f in range(1, Z):
            zc[q, f].wait_recv()
            value = value + zrecv[q, f - 1].astype(F32)
        out[q // JH, :, pl.ds((q % JH) * JW, JW)] = value

    Q = T * JH
    todo.clear()
    step, hop = 10.4 / Q, 22.5 / Q
    for q in range(Q):
        plan(step * (q + 1), stage_a, q)
        plan(step * (q + 2) + 0.1, stage_b, q)
        arrived = 2 * step + 1 + hop * (q + 1) + 1.5
        plan(arrived, stage_c, q)
        plan(arrived + hop + 2.5, stage_d, q)
    for _, _, what, args in sorted(todo, key=lambda item: item[:2]):
        what(*args)
    for copy in sent:
        copy.wait_send()


def local(green, factors, pattern, coulomb):
    n = lax.axis_size("aux")
    T, O, _ = green.shape
    R = factors.shape[0]
    A = n * R
    chips = n // 2
    Z = 4
    X = chips // Z
    JH = 2
    H = 4
    JW = O // JH
    Q = T * JH
    OUT = O // n
    dma = pltpu.SemaphoreType.DMA
    vm = pltpu.VMEM
    scratch = [
        vm((R, O), BF16), vm((A, O), BF16), vm((n, 1, R), F32), vm((T, O, O), BF16),
        vm((T, 2 * R, O), BF16), vm((T, R, O), BF16), vm((R, R), F32), vm((T, R, A), BF16),
        vm((Q, O, JW), F32), vm((Q, chips, OUT, JW), BF16), vm((Q, chips, OUT, JW), BF16),
        vm((Q, X - 1, Z, OUT, JW), BF16), vm((Q, X - 1, Z, OUT, JW), BF16),
        vm((Q, Z - 1, OUT, JW), BF16), vm((Q, Z - 1, OUT, JW), BF16), vm((Q, OUT, JW), F32),
        dma((T,)),
        dma((Z - 1, H)), dma((Z - 1, H)),
        dma((Z, X - 1, H)), dma((Z, X - 1, H)),
        dma((Z, X - 1, H // 2)), dma((Z, X - 1, H // 2)),
        dma((Z, H)), dma((Z, H)),
        dma((Z, X - 1, H)), dma((Z, X - 1, H)),
        dma((Z - 1,)), dma((Z - 1,)), dma((Z, X - 1)), dma((Z, X - 1)),
        dma((Z,)), dma((Z,)), dma((Z, X - 1)), dma((Z, X - 1)),
        dma((T,)), dma((T,)),
        dma((Q,)), dma((Q,)),
        dma((Q, X - 1)), dma((Q, X - 1)),
        dma((Q, Z - 1)), dma((Q, Z - 1)),
    ]
    vmem = pl.BlockSpec(memory_space=pltpu.VMEM)
    result = pl.pallas_call(
        functools.partial(kernel, (Z, X, JH, H)),
        out_shape=jax.ShapeDtypeStruct((T, OUT, O), F32),
        in_specs=[pl.BlockSpec(memory_space=pltpu.SMEM), vmem, vmem,
                  pl.BlockSpec(memory_space=pl.ANY)],
        out_specs=vmem,
        scratch_shapes=scratch,
        compiler_params=pltpu.CompilerParams(
            collective_id=0, has_side_effects=True, vmem_limit_bytes=60 * 2**20),
    )(pattern, factors, coulomb.reshape(1, R), green)
    return jnp.transpose(result, (1, 0, 2))


def solution(mesh):
    in_specs = (P("tm", None, None), P("aux", None), P("aux", None), P("aux"))
    out_specs = P("aux", "tm", None)
    return jax.shard_map(local, mesh=mesh, in_specs=in_specs, out_specs=out_specs, check_vma=False)
```

```python
import functools

import jax
import jax.numpy as jnp
from jax import lax
from jax.experimental import pallas as pl
from jax.experimental.pallas import tpu as pltpu
from jax.sharding import PartitionSpec as P

MESH = pl.DeviceIdType.MESH
F32, BF16 = jnp.float32, jnp.bfloat16


def turned(p):
    return p + lax.div(p, 2) * (1 - 2 * lax.rem(p, 2))


def dot(a, b, da, db):
    return lax.dot_general(a, b, (((da,), (db,)), ((), ())), preferred_element_type=F32)


def kernel(cfg, pattern, factors, coul, green_hbm, out, own, rows, weights, green, left_right,
           own_right, cp, kern, sig, csend, crecv, xsend, xrecv, zsend, zrecv, fin,
           gsem, ring_s, ring_r, x_s, x_r, y_s, y_r, cc_s, cc_r, cx_s, cx_r,
           wring_s, wring_r, wx_s, wx_r, wcc_s, wcc_r, wcx_s, wcx_r, tm_s, tm_r,
           rc_s, rc_r, rx_s, rx_r, rz_s, rz_r):
    Z, X, JH, H = cfg
    T, O = green.shape[0], green.shape[1]
    R = own.shape[0]
    JW = O // JH
    OUT = out.shape[1]
    tms = lax.axis_size("tm")
    a, tmi = lax.axis_index("aux"), lax.axis_index("tm")
    c = lax.rem(a, 2)
    x = lax.rem(lax.div(a, 2), X)
    z = lax.div(a, 2 * X)
    pos = turned(z)

    def dev(z_, x_, c_):
        return (z_ * X + x_) * 2 + c_

    def xo(e):
        return lax.rem(x + e, X)

    def zo(f):
        return lax.rem(z + f, Z)

    partner = lax.rem(tmi + tms // 2, tms)
    plane = lax.rem(tmi, 2)
    mate = tmi + 1 - 2 * plane
    sibling = dev(z, x, 1 - c)
    sent = []

    def send(src, dst, s, r, **where):
        copy = pltpu.make_async_remote_copy(
            src_ref=src, dst_ref=dst, send_sem=s, recv_sem=r,
            device_id=where, device_id_type=MESH)
        copy.start()
        sent.append(copy)
        return copy

    loads = [pltpu.make_async_copy(green_hbm.at[t], green.at[t], gsem.at[t]) for t in range(T)]
    for copy in loads:
        copy.start()

    here = pl.multiple_of(a * R, R)
    brows = R // pattern.shape[0]
    bcols = O // pattern.shape[1]
    for i in range(pattern.shape[0]):
        for j in range(pattern.shape[1]):
            rs, cs = pl.ds(i * brows, brows), pl.ds(j * bcols, bcols)
            own[rs, cs] = (factors[rs, cs].astype(F32) * pattern[i, j].astype(F32)).astype(BF16)
    rows[pl.ds(here, R), :] = own[...]
    weights[a] = coul[...]
    cp[...] = jnp.transpose(jnp.broadcast_to(coul[...], (R, R)))

    barrier = pltpu.get_barrier_semaphore()
    friends = [{"aux": dev(zo(f), x, c)} for f in range(1, Z)]
    friends += [{"aux": dev(z, xo(e), c)} for e in range(1, X)]
    friends += [{"aux": sibling}, {"tm": partner}]
    if tms > 2 and tms % 2 == 0:
        friends += [{"tm": mate}]
    for where in friends:
        pl.semaphore_signal(barrier, inc=1, device_id=where, device_id_type=MESH)
    pl.semaphore_wait(barrier, len(friends))

    nextd = dev(turned(lax.rem(pos + 1, Z)), x, c)
    PR = R // H
    shared = (1,) if tms % 2 == 0 else ()

    def col_owner(k):
        return dev(turned(lax.rem(pos + Z - k, Z)), x, c)

    def xin_owner(k, e):
        return dev(turned(lax.rem(pos + Z - k, Z)), lax.rem(x + X - e, X), c)

    def pass_piece(owner, h, s, r, first=False, **where):
        at = pl.ds(pl.multiple_of(owner * R + h * PR, PR), PR)
        src = own.at[pl.ds(pl.multiple_of(h * PR, PR), PR)] if first else rows.at[at]
        return send(src, rows.at[at], s, r, **where)

    def pass_weight(owner, s, r, first=False, **where):
        return send(coul if first else weights.at[owner], weights.at[owner], s, r, **where)

    ring, xs, ys, ccs, cxs = {}, {}, {}, {}, {}
    wring, wxs, wccs, wcxs = {}, {}, {}, {}

    def wait_all(copies):
        for copy in copies:
            copy.wait_recv()

    def col(k, h):
        if k > 0:
            ring[k, h].wait_recv()
            if h == 0:
                wring[k].wait_recv()
        owner, first = col_owner(k), k == 0
        if k < Z - 1:
            ring[k + 1, h] = pass_piece(owner, h, ring_s.at[k, h], ring_r.at[k, h], first, aux=nextd)
        for e in range(1, X):
            to = dev(z, xo(e), c)
            if k not in shared:
                xs[k, e, h] = pass_piece(owner, h, x_s.at[k, e - 1, h], x_r.at[k, e - 1, h], first,
                                         aux=to)
            elif h % 2:
                i = h // 2
                xs[k, e, i] = pass_piece(owner, 2 * i + plane, x_s.at[k, e - 1, i],
                                         x_r.at[k, e - 1, i], first, aux=to)
        ccs.setdefault(k, []).append(
            pass_piece(owner, h, cc_s.at[k, h], cc_r.at[k, h], first, aux=sibling))
        if h == 0:
            if k < Z - 1:
                wring[k + 1] = pass_weight(owner, wring_s.at[k], wring_r.at[k], first, aux=nextd)
            for e in range(1, X):
                wxs[k, e] = pass_weight(owner, wx_s.at[k, e - 1], wx_r.at[k, e - 1], first,
                                        aux=dev(z, xo(e), c))
            ccs[k].append(pass_weight(owner, wcc_s.at[k], wcc_r.at[k], first, aux=sibling))

    def xin(k, i):
        for e in range(1, X):
            owner = xin_owner(k, e)
            xs[k, e, i].wait_recv()
            h, n = i, i
            if k in shared:
                h, n = 2 * i + plane, 2 * i
                ys[k, e, i] = pass_piece(owner, h, y_s.at[k, e - 1, i], y_r.at[k, e - 1, i], tm=mate)
            mine = cxs.setdefault((k, e), [])
            mine.append(pass_piece(owner, h, cx_s.at[k, e - 1, n], cx_r.at[k, e - 1, n], aux=sibling))
            if i == 0:
                wxs[k, e].wait_recv()
                mine.append(pass_weight(owner, wcx_s.at[k, e - 1], wcx_r.at[k, e - 1], aux=sibling))

    def yin(k, i):
        for e in range(1, X):
            ys[k, e, i].wait_recv()
            cxs[k, e].append(
                pass_piece(xin_owner(k, e), 2 * i + 1 - plane, cx_s.at[k, e - 1, 2 * i + 1],
                           cx_r.at[k, e - 1, 2 * i + 1], aux=sibling))

    waited = set()

    def once(key, copies):
        if key not in waited:
            waited.add(key)
            wait_all(copies)

    def blocks(owner, ts):
        def one(i, carry):
            who = owner - c + lax.rem(c + lax.div(i, len(ts)), 2)
            t = ts[0] + lax.rem(i, len(ts))
            at = pl.ds(pl.multiple_of(who * R, R), R)
            both = dot(left_right[t], rows[at, :], 1, 1)
            ag, mirror = both[:R], both[R:]
            kern[t, :, at] = (ag * ag * mirror * (cp[...] * weights[who])).astype(BF16)
            return carry
        lax.fori_loop(0, 2 * len(ts), one, 0)

    def do_col(k, ts):
        once(("c", k), ccs[k])
        blocks(col_owner(k), ts)

    def do_xin(k, ts):
        for e in range(1, X):
            once(("x", k, e), cxs[k, e])
            blocks(xin_owner(k, e), ts)

    rights = {}

    def project_right(t):
        loads[t].wait()

        def one(j, carry):
            at = pl.ds(pl.multiple_of(j * 256, 256), 256)
            own_right[t, :, at] = dot(own[...], green[t, at, :], 1, 1).astype(BF16)
            return carry
        lax.fori_loop(0, O // 256, one, 0)
        rights[t] = send(own_right.at[t], left_right.at[t, pl.ds(R, R)], tm_s.at[t], tm_r.at[t],
                         tm=partner)

    def project_left(t):
        def one(j, carry):
            at = pl.ds(pl.multiple_of(j * 256, 256), 256)
            left_right[t, pl.ds(0, R), at] = dot(own[...], green[t, :, at], 1, 0).astype(BF16)
            return carry
        lax.fori_loop(0, O // 256, one, 0)

    for h in range(H):
        col(0, h)
    for t in range(T):
        project_right(t)
    for t in range(T):
        project_left(t)

    rest, every = tuple(range(1, T)), tuple(range(T))
    todo = []

    def plan(when, what, *args):
        todo.append((when, len(todo), what, args))

    lag = 0.7
    for k in range(1, Z):
        for h in range(H):
            plan((k - 1) * H + h + 1 + lag * k, col, k, h)
    last = 0.0
    for k in range(Z):
        if k in shared:
            for i in range(H // 2):
                ready = (k - 1) * H + 2 * i + 2 + lag * k
                last = max(last + 1, ready + 1 + lag)
                plan(last, xin, k, i)
                plan(max(last + 1 + lag, 11.7 + i), yin, k, i)
        else:
            for i in range(H):
                last = k * H + i + 1 + lag
                plan(last, xin, k, i)
    plan(6.5, lambda: rights[0].wait_recv())
    plan(6.6, do_col, 0, (0,))
    plan(6.7, do_col, 1, (0,))
    plan(6.8, do_xin, 0, (0,))
    plan(13.3, do_xin, 1, (0,))
    plan(9.6, do_col, 2, (0,))
    plan(10.6, lambda: [rights[t].wait_recv() for t in rest])
    plan(10.61, do_col, 0, rest)
    plan(10.8, do_col, 1, rest)
    plan(11.2, do_xin, 0, rest)
    plan(13.35, do_xin, 1, rest)
    plan(12.3, do_col, 2, rest)
    tail = 13.3
    for k in range(2, Z):
        if k > 2:
            plan(max(tail, (k - 1) * H + H + lag * k + 0.5), do_col, k, every)
        full = max([w for w, _, f, g in todo if f in (xin, yin) and g[0] == k])
        plan(full + 0.4, do_xin, k, every)
    for _, _, what, args in sorted(todo, key=lambda item: item[:2]):
        what(*args)

    pairs = Z * X
    cross, xc, zc = {}, {}, {}

    def stage_a(q):
        t, j0 = q // JH, (q % JH) * JW

        def one(j, carry):
            at = pl.ds(pl.multiple_of(j0 + j * 256, 256), 256)
            carried = dot(kern[t], rows[:, at], 1, 0).astype(BF16)
            to = pl.ds(pl.multiple_of(j * 256, 256), 256)
            sig[q, :, to] = dot(own[...], carried, 0, 0)
            return carry
        lax.fori_loop(0, JW // 256, one, 0)
        for g in range(pairs):
            at = pl.ds(pl.multiple_of((g * 2 + 1 - c) * OUT, OUT), OUT)
            csend[q, g] = sig[q, at, :].astype(BF16)
        cross[q] = send(csend.at[q], crecv.at[q], rc_s.at[q], rc_r.at[q], aux=sibling)

    def summed(q, g):
        at = pl.ds(pl.multiple_of((g * 2 + c) * OUT, OUT), OUT)
        return sig[q, at, :] + crecv[q, g].astype(F32)

    def stage_b(q):
        cross[q].wait_recv()
        for e in range(1, X):
            for zz in range(Z):
                xsend[q, e - 1, zz] = summed(q, zz * X + xo(e)).astype(BF16)
            xc[q, e] = send(xsend.at[q, e - 1], xrecv.at[q, e - 1], rx_s.at[q, e - 1],
                            rx_r.at[q, e - 1], aux=dev(z, xo(e), c))

    def stage_c(q):
        for e in range(1, X):
            xc[q, e].wait_recv()
        for f in list(range(1, Z)) + [0]:
            value = summed(q, zo(f) * X + x)
            for e in range(1, X):
                value = value + xrecv[q, e - 1, zo(f)].astype(F32)
            if f == 0:
                fin[q] = value
            else:
                zsend[q, f - 1] = value.astype(BF16)
                zc[q, f] = send(zsend.at[q, f - 1], zrecv.at[q, f - 1], rz_s.at[q, f - 1],
                                rz_r.at[q, f - 1], aux=dev(zo(f), x, c))

    def stage_d(q):
        value = fin[q]
        for f in range(1, Z):
            zc[q, f].wait_recv()
            value = value + zrecv[q, f - 1].astype(F32)
        out[q // JH, :, pl.ds((q % JH) * JW, JW)] = value

    Q = T * JH
    todo.clear()
    step, hop = 10.4 / Q, 22.5 / Q
    for q in range(Q):
        plan(step * (q + 1), stage_a, q)
        plan(step * (q + 2) + 0.1, stage_b, q)
        arrived = 2 * step + 1 + hop * (q + 1) + 1.5
        plan(arrived, stage_c, q)
        plan(arrived + hop + 2.5, stage_d, q)
    for _, _, what, args in sorted(todo, key=lambda item: item[:2]):
        what(*args)
    for copy in sent:
        copy.wait_send()


def local(green, factors, pattern, coulomb):
    n = lax.axis_size("aux")
    T, O, _ = green.shape
    R = factors.shape[0]
    A = n * R
    chips = n // 2
    Z = 4
    X = chips // Z
    JH = 2
    H = 4
    JW = O // JH
    Q = T * JH
    OUT = O // n
    dma = pltpu.SemaphoreType.DMA
    vm = pltpu.VMEM
    scratch = [
        vm((R, O), BF16), vm((A, O), BF16), vm((n, 1, R), F32), vm((T, O, O), BF16),
        vm((T, 2 * R, O), BF16), vm((T, R, O), BF16), vm((R, R), F32), vm((T, R, A), BF16),
        vm((Q, O, JW), F32), vm((Q, chips, OUT, JW), BF16), vm((Q, chips, OUT, JW), BF16),
        vm((Q, X - 1, Z, OUT, JW), BF16), vm((Q, X - 1, Z, OUT, JW), BF16),
        vm((Q, Z - 1, OUT, JW), BF16), vm((Q, Z - 1, OUT, JW), BF16), vm((Q, OUT, JW), F32),
        dma((T,)),
        dma((Z - 1, H)), dma((Z - 1, H)),
        dma((Z, X - 1, H)), dma((Z, X - 1, H)),
        dma((Z, X - 1, H // 2)), dma((Z, X - 1, H // 2)),
        dma((Z, H)), dma((Z, H)),
        dma((Z, X - 1, H)), dma((Z, X - 1, H)),
        dma((Z - 1,)), dma((Z - 1,)), dma((Z, X - 1)), dma((Z, X - 1)),
        dma((Z,)), dma((Z,)), dma((Z, X - 1)), dma((Z, X - 1)),
        dma((T,)), dma((T,)),
        dma((Q,)), dma((Q,)),
        dma((Q, X - 1)), dma((Q, X - 1)),
        dma((Q, Z - 1)), dma((Q, Z - 1)),
    ]
    vmem = pl.BlockSpec(memory_space=pltpu.VMEM)
    result = pl.pallas_call(
        functools.partial(kernel, (Z, X, JH, H)),
        out_shape=jax.ShapeDtypeStruct((T, OUT, O), F32),
        in_specs=[pl.BlockSpec(memory_space=pltpu.SMEM), vmem, vmem,
                  pl.BlockSpec(memory_space=pl.ANY)],
        out_specs=vmem,
        scratch_shapes=scratch,
        compiler_params=pltpu.CompilerParams(
            collective_id=0, has_side_effects=True, vmem_limit_bytes=60 * 2**20),
    )(pattern, factors, coulomb.reshape(1, R), green)
    return jnp.transpose(result, (1, 0, 2))


def solution(mesh):
    in_specs = (P("tm", None, None), P("aux", None), P("aux", None), P("aux"))
    out_specs = P("aux", "tm", None)
    return jax.shard_map(local, mesh=mesh, in_specs=in_specs, out_specs=out_specs, check_vma=False)
```

```python
import functools

import jax
import jax.numpy as jnp
from jax import lax
from jax.experimental import pallas as pl
from jax.experimental.pallas import tpu as pltpu
from jax.sharding import PartitionSpec as P

MESH = pl.DeviceIdType.MESH
F32, BF16 = jnp.float32, jnp.bfloat16


def turned(p):
    return p + lax.div(p, 2) * (1 - 2 * lax.rem(p, 2))


def dot(a, b, da, db):
    return lax.dot_general(a, b, (((da,), (db,)), ((), ())), preferred_element_type=F32)


def kernel(cfg, pattern, factors, coul, green_hbm, out, own, rows, weights, green, left_right,
           own_right, cp, kern, sig, csend, crecv, xsend, xrecv, zsend, zrecv, fin,
           gsem, ring_s, ring_r, x_s, x_r, y_s, y_r, cc_s, cc_r, cx_s, cx_r,
           wring_s, wring_r, wx_s, wx_r, wcc_s, wcc_r, wcx_s, wcx_r, tm_s, tm_r,
           rc_s, rc_r, rx_s, rx_r, rz_s, rz_r):
    Z, X, JH, H = cfg
    T, O = green.shape[0], green.shape[1]
    R = own.shape[0]
    JW = O // JH
    OUT = out.shape[0]
    tms = lax.axis_size("tm")
    a, tmi = lax.axis_index("aux"), lax.axis_index("tm")
    c = lax.rem(a, 2)
    x = lax.rem(lax.div(a, 2), X)
    z = lax.div(a, 2 * X)
    pos = turned(z)

    def dev(z_, x_, c_):
        return (z_ * X + x_) * 2 + c_

    def xo(e):
        return lax.rem(x + e, X)

    def zo(f):
        return lax.rem(z + f, Z)

    partner = lax.rem(tmi + tms // 2, tms)
    plane = lax.rem(tmi, 2)
    mate = tmi + 1 - 2 * plane
    sibling = dev(z, x, 1 - c)
    sent = []

    def send(src, dst, s, r, **where):
        copy = pltpu.make_async_remote_copy(
            src_ref=src, dst_ref=dst, send_sem=s, recv_sem=r,
            device_id=where, device_id_type=MESH)
        copy.start()
        sent.append(copy)
        return copy

    loads = [pltpu.make_async_copy(green_hbm.at[t], green.at[t], gsem.at[t]) for t in range(T)]
    for copy in loads:
        copy.start()

    here = pl.multiple_of(a * R, R)
    brows = R // pattern.shape[0]
    bcols = O // pattern.shape[1]
    for i in range(pattern.shape[0]):
        for j in range(pattern.shape[1]):
            rs, cs = pl.ds(i * brows, brows), pl.ds(j * bcols, bcols)
            own[rs, cs] = (factors[rs, cs].astype(F32) * pattern[i, j].astype(F32)).astype(BF16)
    rows[pl.ds(here, R), :] = own[...]
    weights[a] = coul[...]
    cp[...] = jnp.transpose(jnp.broadcast_to(coul[...], (R, R)))

    barrier = pltpu.get_barrier_semaphore()
    friends = [{"aux": dev(zo(f), x, c)} for f in range(1, Z)]
    friends += [{"aux": dev(z, xo(e), c)} for e in range(1, X)]
    friends += [{"aux": sibling}, {"tm": partner}]
    if tms > 2 and tms % 2 == 0:
        friends += [{"tm": mate}]
    for where in friends:
        pl.semaphore_signal(barrier, inc=1, device_id=where, device_id_type=MESH)
    pl.semaphore_wait(barrier, len(friends))

    nextd = dev(turned(lax.rem(pos + 1, Z)), x, c)
    PR = R // H
    shared = (1,) if tms % 2 == 0 else ()

    def col_owner(k):
        return dev(turned(lax.rem(pos + Z - k, Z)), x, c)

    def xin_owner(k, e):
        return dev(turned(lax.rem(pos + Z - k, Z)), lax.rem(x + X - e, X), c)

    def pass_piece(owner, h, s, r, first=False, **where):
        at = pl.ds(pl.multiple_of(owner * R + h * PR, PR), PR)
        src = own.at[pl.ds(pl.multiple_of(h * PR, PR), PR)] if first else rows.at[at]
        return send(src, rows.at[at], s, r, **where)

    def pass_weight(owner, s, r, first=False, **where):
        return send(coul if first else weights.at[owner], weights.at[owner], s, r, **where)

    ring, xs, ys, ccs, cxs = {}, {}, {}, {}, {}
    wring, wxs, wccs, wcxs = {}, {}, {}, {}

    def wait_all(copies):
        for copy in copies:
            copy.wait_recv()

    def col(k, h):
        if k > 0:
            ring[k, h].wait_recv()
            if h == 0:
                wring[k].wait_recv()
        owner, first = col_owner(k), k == 0
        if k < Z - 1:
            ring[k + 1, h] = pass_piece(owner, h, ring_s.at[k, h], ring_r.at[k, h], first, aux=nextd)
        for e in range(1, X):
            to = dev(z, xo(e), c)
            if k not in shared:
                xs[k, e, h] = pass_piece(owner, h, x_s.at[k, e - 1, h], x_r.at[k, e - 1, h], first,
                                         aux=to)
            elif h % 2:
                i = h // 2
                xs[k, e, i] = pass_piece(owner, 2 * i + plane, x_s.at[k, e - 1, i],
                                         x_r.at[k, e - 1, i], first, aux=to)
        ccs.setdefault(k, []).append(
            pass_piece(owner, h, cc_s.at[k, h], cc_r.at[k, h], first, aux=sibling))
        if h == 0:
            if k < Z - 1:
                wring[k + 1] = pass_weight(owner, wring_s.at[k], wring_r.at[k], first, aux=nextd)
            for e in range(1, X):
                wxs[k, e] = pass_weight(owner, wx_s.at[k, e - 1], wx_r.at[k, e - 1], first,
                                        aux=dev(z, xo(e), c))
            ccs[k].append(pass_weight(owner, wcc_s.at[k], wcc_r.at[k], first, aux=sibling))

    def xin(k, i):
        for e in range(1, X):
            owner = xin_owner(k, e)
            xs[k, e, i].wait_recv()
            h, n = i, i
            if k in shared:
                h, n = 2 * i + plane, 2 * i
                ys[k, e, i] = pass_piece(owner, h, y_s.at[k, e - 1, i], y_r.at[k, e - 1, i], tm=mate)
            mine = cxs.setdefault((k, e), [])
            mine.append(pass_piece(owner, h, cx_s.at[k, e - 1, n], cx_r.at[k, e - 1, n], aux=sibling))
            if i == 0:
                wxs[k, e].wait_recv()
                mine.append(pass_weight(owner, wcx_s.at[k, e - 1], wcx_r.at[k, e - 1], aux=sibling))

    def yin(k, i):
        for e in range(1, X):
            ys[k, e, i].wait_recv()
            cxs[k, e].append(
                pass_piece(xin_owner(k, e), 2 * i + 1 - plane, cx_s.at[k, e - 1, 2 * i + 1],
                           cx_r.at[k, e - 1, 2 * i + 1], aux=sibling))

    waited = set()

    def once(key, copies):
        if key not in waited:
            waited.add(key)
            wait_all(copies)

    def blocks(owner, ts):
        def one(i, carry):
            who = owner - c + lax.rem(c + lax.div(i, len(ts)), 2)
            t = ts[0] + lax.rem(i, len(ts))
            at = pl.ds(pl.multiple_of(who * R, R), R)
            both = dot(left_right[t], rows[at, :], 1, 1)
            ag, mirror = both[:R], both[R:]
            kern[t, :, at] = (ag * ag * mirror * (cp[...] * weights[who])).astype(BF16)
            return carry
        lax.fori_loop(0, 2 * len(ts), one, 0)

    def do_col(k, ts):
        once(("c", k), ccs[k])
        blocks(col_owner(k), ts)

    def do_xin(k, ts):
        for e in range(1, X):
            once(("x", k, e), cxs[k, e])
            blocks(xin_owner(k, e), ts)

    rights = {}

    def project_right(t):
        loads[t].wait()

        def one(j, carry):
            at = pl.ds(pl.multiple_of(j * 256, 256), 256)
            own_right[t, :, at] = dot(own[...], green[t, at, :], 1, 1).astype(BF16)
            return carry
        lax.fori_loop(0, O // 256, one, 0)
        rights[t] = send(own_right.at[t], left_right.at[t, pl.ds(R, R)], tm_s.at[t], tm_r.at[t],
                         tm=partner)

    def project_left(t):
        def one(j, carry):
            at = pl.ds(pl.multiple_of(j * 256, 256), 256)
            left_right[t, pl.ds(0, R), at] = dot(own[...], green[t, :, at], 1, 0).astype(BF16)
            return carry
        lax.fori_loop(0, O // 256, one, 0)

    for h in range(H):
        col(0, h)
    for t in range(T):
        project_right(t)
    for t in range(T):
        project_left(t)

    rest, every = tuple(range(1, T)), tuple(range(T))
    todo = []

    def plan(when, what, *args):
        todo.append((when, len(todo), what, args))

    lag = 0.7
    for k in range(1, Z):
        for h in range(H):
            plan((k - 1) * H + h + 1 + lag * k, col, k, h)
    last = 0.0
    for k in range(Z):
        if k in shared:
            for i in range(H // 2):
                ready = (k - 1) * H + 2 * i + 2 + lag * k
                last = max(last + 1, ready + 1 + lag)
                plan(last, xin, k, i)
                plan(max(last + 1 + lag, 11.7 + i), yin, k, i)
        else:
            for i in range(H):
                last = k * H + i + 1 + lag
                plan(last, xin, k, i)
    plan(6.5, lambda: rights[0].wait_recv())
    plan(6.6, do_col, 0, (0,))
    plan(6.7, do_col, 1, (0,))
    plan(6.8, do_xin, 0, (0,))
    plan(13.3, do_xin, 1, (0,))
    plan(9.6, do_col, 2, (0,))
    plan(10.6, lambda: [rights[t].wait_recv() for t in rest])
    plan(10.61, do_col, 0, rest)
    plan(10.8, do_col, 1, rest)
    plan(11.2, do_xin, 0, rest)
    plan(13.35, do_xin, 1, rest)
    plan(12.3, do_col, 2, rest)
    tail = 13.3
    for k in range(2, Z):
        if k > 2:
            plan(max(tail, (k - 1) * H + H + lag * k + 0.5), do_col, k, every)
        full = max([w for w, _, f, g in todo if f in (xin, yin) and g[0] == k])
        plan(full + 0.4, do_xin, k, every)
    for _, _, what, args in sorted(todo, key=lambda item: item[:2]):
        what(*args)

    pairs = Z * X
    cross, xc, zc = {}, {}, {}

    def stage_a(q):
        t, j0 = q // JH, (q % JH) * JW

        def one(j, carry):
            at = pl.ds(pl.multiple_of(j0 + j * 256, 256), 256)
            carried = dot(kern[t], rows[:, at], 1, 0).astype(BF16)
            to = pl.ds(pl.multiple_of(j * 256, 256), 256)
            sig[q, :, to] = dot(own[...], carried, 0, 0)
            return carry
        lax.fori_loop(0, JW // 256, one, 0)
        for g in range(pairs):
            at = pl.ds(pl.multiple_of((g * 2 + 1 - c) * OUT, OUT), OUT)
            csend[q, g] = sig[q, at, :].astype(BF16)
        cross[q] = send(csend.at[q], crecv.at[q], rc_s.at[q], rc_r.at[q], aux=sibling)

    def summed(q, g):
        at = pl.ds(pl.multiple_of((g * 2 + c) * OUT, OUT), OUT)
        return sig[q, at, :] + crecv[q, g].astype(F32)

    def stage_b(q):
        cross[q].wait_recv()
        for e in range(1, X):
            for zz in range(Z):
                xsend[q, e - 1, zz] = summed(q, zz * X + xo(e)).astype(BF16)
            xc[q, e] = send(xsend.at[q, e - 1], xrecv.at[q, e - 1], rx_s.at[q, e - 1],
                            rx_r.at[q, e - 1], aux=dev(z, xo(e), c))

    def stage_c(q):
        for e in range(1, X):
            xc[q, e].wait_recv()
        for f in list(range(1, Z)) + [0]:
            value = summed(q, zo(f) * X + x)
            for e in range(1, X):
                value = value + xrecv[q, e - 1, zo(f)].astype(F32)
            if f == 0:
                fin[q] = value
            else:
                zsend[q, f - 1] = value.astype(BF16)
                zc[q, f] = send(zsend.at[q, f - 1], zrecv.at[q, f - 1], rz_s.at[q, f - 1],
                                rz_r.at[q, f - 1], aux=dev(zo(f), x, c))

    def stage_d(q):
        value = fin[q]
        for f in range(1, Z):
            zc[q, f].wait_recv()
            value = value + zrecv[q, f - 1].astype(F32)
        out[:, q // JH, pl.ds((q % JH) * JW, JW)] = value

    Q = T * JH
    todo.clear()
    step, hop = 10.4 / Q, 22.5 / Q
    for q in range(Q):
        plan(step * (q + 1), stage_a, q)
        plan(step * (q + 2) + 0.1, stage_b, q)
        arrived = 2 * step + 1 + hop * (q + 1) + 1.5
        plan(arrived, stage_c, q)
        plan(arrived + hop + 2.5, stage_d, q)
    for _, _, what, args in sorted(todo, key=lambda item: item[:2]):
        what(*args)
    for copy in sent:
        copy.wait_send()


def local(green, factors, pattern, coulomb):
    n = lax.axis_size("aux")
    T, O, _ = green.shape
    R = factors.shape[0]
    A = n * R
    chips = n // 2
    Z = 4
    X = chips // Z
    JH = 2
    H = 4
    JW = O // JH
    Q = T * JH
    OUT = O // n
    dma = pltpu.SemaphoreType.DMA
    vm = pltpu.VMEM
    scratch = [
        vm((R, O), BF16), vm((A, O), BF16), vm((n, 1, R), F32), vm((T, O, O), BF16),
        vm((T, 2 * R, O), BF16), vm((T, R, O), BF16), vm((R, R), F32), vm((T, R, A), BF16),
        vm((Q, O, JW), F32), vm((Q, chips, OUT, JW), BF16), vm((Q, chips, OUT, JW), BF16),
        vm((Q, X - 1, Z, OUT, JW), BF16), vm((Q, X - 1, Z, OUT, JW), BF16),
        vm((Q, Z - 1, OUT, JW), BF16), vm((Q, Z - 1, OUT, JW), BF16), vm((Q, OUT, JW), F32),
        dma((T,)),
        dma((Z - 1, H)), dma((Z - 1, H)),
        dma((Z, X - 1, H)), dma((Z, X - 1, H)),
        dma((Z, X - 1, H // 2)), dma((Z, X - 1, H // 2)),
        dma((Z, H)), dma((Z, H)),
        dma((Z, X - 1, H)), dma((Z, X - 1, H)),
        dma((Z - 1,)), dma((Z - 1,)), dma((Z, X - 1)), dma((Z, X - 1)),
        dma((Z,)), dma((Z,)), dma((Z, X - 1)), dma((Z, X - 1)),
        dma((T,)), dma((T,)),
        dma((Q,)), dma((Q,)),
        dma((Q, X - 1)), dma((Q, X - 1)),
        dma((Q, Z - 1)), dma((Q, Z - 1)),
    ]
    vmem = pl.BlockSpec(memory_space=pltpu.VMEM)
    result = pl.pallas_call(
        functools.partial(kernel, (Z, X, JH, H)),
        out_shape=jax.ShapeDtypeStruct((OUT, T, O), F32),
        in_specs=[pl.BlockSpec(memory_space=pltpu.SMEM), vmem, vmem,
                  pl.BlockSpec(memory_space=pl.ANY)],
        out_specs=vmem,
        scratch_shapes=scratch,
        compiler_params=pltpu.CompilerParams(
            collective_id=0, has_side_effects=True, vmem_limit_bytes=60 * 2**20),
    )(pattern, factors, coulomb.reshape(1, R), green)
    return result


def solution(mesh):
    in_specs = (P("tm", None, None), P("aux", None), P("aux", None), P("aux"))
    out_specs = P("aux", "tm", None)
    return jax.shard_map(local, mesh=mesh, in_specs=in_specs, out_specs=out_specs, check_vma=False)
```
